256 devices in a mesh: row: 16 (over x, y_hi, core), col: 16 (over z, y_lo).
Axes of the slice: x: 4, y: 4 (y_hi: 2, y_lo: 2; y = y_hi * 2 + y_lo), z: 8, core: 2. Of those that a mesh axis runs over, the one named last changes fastest.
Arguments:
- image: float32 [2048, 2048], P('row', 'col'), may hold values from -10.1 to 10.1
Outputs:
- features: bfloat16 [12, 2048, 2048], P(None, 'row', 'col')
The draws below stay inside these ranges and needn't reach their ends.
All inputs are finite; a program needn't handle non-finite values.
Results may differ from the reference program's by a relative error of at most 0.0014.
Values sent between devices are 32-bit elements; how exact they have to be, the bound alone decides.
A program may use at most 64 MiB of HBM per device.

```python
import math
import jax
import jax.numpy as jnp
from jax import lax

SIG_A = 128
SIG_B = 256
HEIGHT = 2048
WIDTH = 2048


def draw_image(key, part):
    first_key, second_key = jax.random.split(key)
    rough = jnp.clip(jax.random.normal(first_key, (HEIGHT, WIDTH), jnp.float32), -5.0, 5.0)
    factor = jnp.exp(jax.random.uniform(second_key, (HEIGHT, WIDTH), jnp.float32, math.log(0.5), math.log(2.0)))
    result = rough * factor
    return result


def setup_inputs(seed: int = 0) -> dict:
    key_list = jax.random.split(jax.random.key(seed), 2)
    return {
        "image": draw_image(jax.random.fold_in(key_list[1], 71), 0),
    }


DER_FIRST = (1.0 / 280, -4.0 / 105, 1.0 / 5, -4.0 / 5, 0.0, 4.0 / 5, -1.0 / 5, 4.0 / 105, -1.0 / 280)
DER_SECOND = (-1.0 / 560, 8.0 / 315, -1.0 / 5, 8.0 / 5, -205.0 / 72, 8.0 / 5, -1.0 / 5, 8.0 / 315, -1.0 / 560)
DERICHE_POLES = ((1.68, 3.735, 1.783, 0.6318), (-0.6803, -0.2598, 1.723, 1.997))

def pole_values(deviation):
    normal_sum = 0.0
    for cos_weight, sin_weight, decay, freq in DERICHE_POLES:
        magnitude = math.exp(-decay / deviation)
        real_z = magnitude * math.cos(freq / deviation)
        imag_z = magnitude * math.sin(freq / deviation)
        denom = (1.0 - real_z) ** 2 + imag_z ** 2
        real_q = (real_z - magnitude * magnitude) / denom
        imag_q = imag_z / denom
        normal_sum += cos_weight + 2.0 * (cos_weight * real_q + sin_weight * imag_q)
    pole_list = []
    center = 0.0
    for cos_weight, sin_weight, decay, freq in DERICHE_POLES:
        pole_list.append((cos_weight / normal_sum, -sin_weight / normal_sum, decay / deviation, freq / deviation))
        center += cos_weight / normal_sum
    return (center, pole_list)

def smooth_first(field, deviation):
    center, pole_list = pole_values(deviation)
    shape_tail = (1,) * (field.ndim - 1)
    real_z = []
    imag_z = []
    real_b = []
    imag_b = []
    for real_a, imag_a, rate, freq in pole_list:
        zr = math.exp(-rate) * math.cos(freq)
        zi = math.exp(-rate) * math.sin(freq)
        real_z.append(zr)
        imag_z.append(zi)
        real_b.append(real_a * zr - imag_a * zi)
        imag_b.append(real_a * zi + imag_a * zr)
    real_z = jnp.array(real_z, field.dtype).reshape((2,) + shape_tail)
    imag_z = jnp.array(imag_z, field.dtype).reshape((2,) + shape_tail)
    real_b = jnp.array(real_b, field.dtype).reshape((2,) + shape_tail)
    imag_b = jnp.array(imag_b, field.dtype).reshape((2,) + shape_tail)

    def advance(carry, line):
        state_re, state_im = carry
        emitted = lax.optimization_barrier(jnp.sum(real_b * state_re - imag_b * state_im, axis=0))
        next_re = real_z * state_re - imag_z * state_im + line[None]
        next_im = real_z * state_im + imag_z * state_re
        return ((next_re, next_im), emitted)
    start = jnp.zeros((2,) + field.shape[1:], field.dtype)
    _, causal = lax.scan(advance, (start, start), field)
    _, anticausal = lax.scan(advance, (start, start), field, reverse=True)
    return center * field + causal + anticausal

def tap_sum(source, coeffs, axis, length):
    accum = coeffs[0] * lax.slice_in_dim(source, 0, length, axis=axis)
    for offset in range(1, 9):
        accum = accum + coeffs[offset] * lax.slice_in_dim(source, offset, offset + length, axis=axis)
    return accum

def derivative_fields(padded, rows, cols):
    along_cols = tap_sum(padded, DER_FIRST, 1, cols)
    center = padded[4:4 + rows, 4:4 + cols]
    grad_x = along_cols[4:4 + rows]
    grad_y = tap_sum(padded[:, 4:4 + cols], DER_FIRST, 0, rows)
    curve_xx = tap_sum(padded[4:4 + rows], DER_SECOND, 1, cols)
    curve_xy = tap_sum(along_cols, DER_FIRST, 0, rows)
    curve_yy = tap_sum(padded[:, 4:4 + cols], DER_SECOND, 0, rows)
    return jnp.stack([center, grad_x, grad_y, curve_xx, curve_xy, curve_yy])

def reference(image):
    rows, cols = image.shape
    padded = jnp.pad(image, 4)
    fields = derivative_fields(padded, rows, cols)
    results = []
    for deviation in (SIG_A, SIG_B):
        across = jnp.transpose(smooth_first(jnp.transpose(fields, (2, 0, 1)), deviation), (1, 2, 0))
        downward = jnp.transpose(smooth_first(jnp.transpose(across, (1, 0, 2)), deviation), (1, 0, 2))
        base = 2.0 * math.sqrt(math.pi) * deviation
        factors = jnp.array([base, base * deviation, base * deviation, base * deviation ** 2, base * deviation ** 2, base * deviation ** 2], jnp.float32)
        results.append(downward * factors[:, None, None])
    return jnp.concatenate(results, axis=0).astype(jnp.bfloat16)
```

```python
import functools
import math

import jax
import jax.numpy as jnp
import numpy as np
from jax import lax
from jax.experimental import pallas as pl
from jax.experimental.pallas import tpu as pltpu
from jax.sharding import PartitionSpec as P

SCALES = (128, 256)
DER_FIRST = (1.0 / 280, -4.0 / 105, 1.0 / 5, -4.0 / 5, 0.0, 4.0 / 5, -1.0 / 5, 4.0 / 105, -1.0 / 280)
DER_SECOND = (-1.0 / 560, 8.0 / 315, -1.0 / 5, 8.0 / 5, -205.0 / 72, 8.0 / 5, -1.0 / 5, 8.0 / 315, -1.0 / 560)
DER_NONE = (0.0, 0.0, 0.0, 0.0, 1.0, 0.0, 0.0, 0.0, 0.0)
DERS = (DER_NONE, DER_FIRST, DER_SECOND)
DERICHE_POLES = ((1.68, 3.735, 1.783, 0.6318), (-0.6803, -0.2598, 1.723, 1.997))
FEATURES = ((0, 0), (0, 1), (1, 0), (0, 2), (1, 1), (2, 0))
N = 128
EXT = 64
MESH = pl.DeviceIdType.MESH


def poles(deviation):
    total = 0.0
    for cw, sw, decay, freq in DERICHE_POLES:
        z = np.exp(complex(-decay, freq) / deviation)
        q = z / (1.0 - z)
        total += cw + 2.0 * (cw * q.real + sw * q.imag)
    return [
        (complex(cw, -sw) / total, np.exp(complex(-decay, freq) / deviation))
        for cw, sw, decay, freq in DERICHE_POLES
    ]


def kernel_values(deviation, offsets):
    offsets = np.abs(np.asarray(offsets, dtype=np.float64))
    return sum((a * z**offsets).real for a, z in poles(deviation))


def summary_table():
    table = np.zeros((24, N))
    n = np.arange(N)
    row = 0
    for s in SCALES:
        for _, z in poles(s):
            causal, anti = z ** (N - 1 - n), z**n
            table[row], table[row + 1] = causal.real, causal.imag
            table[16 + row], table[17 + row] = anti.real, anti.imag
            row += 2
    for k in range(4):
        table[8 + k, k] = 1.0
        table[12 + k, N - 4 + k] = 1.0
    return table


def combine_table(count):
    table = np.zeros((count, EXT, count * 16))
    for pos in range(count):
        w = table[pos]
        for k in range(4):
            if pos > 0:
                w[k, (pos - 1) * 16 + 8 + 4 + k] = 1.0
            if pos < count - 1:
                w[4 + k, (pos + 1) * 16 + k] = 1.0
        for si, s in enumerate(SCALES):
            for ai, der in enumerate(DERS):
                for pi, (_, z) in enumerate(poles(s)):
                    up = 8 + (si * 3 + ai) * 8 + pi * 2
                    down = up + 4
                    col = si * 4 + pi * 2
                    dz = sum(der[t + 4] * z**t for t in range(-4, 5))
                    dinv = sum(der[t + 4] * z ** (-t) for t in range(-4, 5))
                    for src in range(count):
                        if src < pos:
                            g = dz * z ** (N * (pos - 1 - src))
                            at = src * 16 + col
                            w[up, at], w[up, at + 1] = g.real, -g.imag
                            w[up + 1, at], w[up + 1, at + 1] = g.imag, g.real
                        if src > pos:
                            g = dinv * z ** (N * (src - pos - 1))
                            at = src * 16 + 8 + col
                            w[down, at], w[down, at + 1] = g.real, -g.imag
                            w[down + 1, at], w[down + 1, at + 1] = g.imag, g.real
                    first = 8
                    last = (count - 1) * 16 + (8 + 4 if pos == count - 1 else 4)
                    for n in range(4):
                        g = -sum(
                            der[n - m + 4] * z ** (N * pos - 1 - m)
                            for m in range(-4, 0)
                            if -4 <= n - m <= 4
                        )
                        w[up, first + n] += g.real
                        w[up + 1, first + n] += g.imag
                        g = -sum(
                            der[n - 4 - m + 4] * z ** (N * (count - 1 - pos) + m)
                            for m in range(0, 4)
                            if -4 <= n - 4 - m <= 4
                        )
                        w[down, last + n] += g.real
                        w[down + 1, last + n] += g.imag
    return table


def filter_tables():
    local = np.zeros((6, N, N))
    ext = np.zeros((6, N, EXT))
    c = np.arange(N)
    for si, s in enumerate(SCALES):
        base = 2.0 * math.sqrt(math.pi) * s
        for ai, der in enumerate(DERS):
            k = si * 3 + ai
            factor = math.sqrt(base) * float(s) ** ai

            def kappa(d):
                return sum(der[t + 4] * kernel_values(s, d + t) for t in range(-4, 5))

            local[k] = kappa(c[:, None] - c[None, :])
            for n in range(4):
                up, down = n - 4, N + n
                ext[k, :, n] = kappa(c - up)
                ext[k, :, 4 + n] = kappa(c - down)
                for a, z in poles(s):
                    dz = sum(der[t + 4] * z**t for t in range(-4, 5))
                    dinv = sum(der[t + 4] * z ** (-t) for t in range(-4, 5))
                    ext[k, :, n] -= (a * dz * z ** (c - up + 0.0)).real
                    ext[k, :, 4 + n] -= (a * dinv * z ** (down - c + 0.0)).real
                ext[k, 4:, n] = 0.0
                ext[k, : N - 4, 4 + n] = 0.0
            for pi, (a, z) in enumerate(poles(s)):
                up = 8 + k * 8 + pi * 2
                g = a * z ** (c + 1.0)
                ext[k, :, up], ext[k, :, up + 1] = g.real, -g.imag
                g = a * z ** (N - c + 0.0)
                ext[k, :, up + 4], ext[k, :, up + 5] = g.real, -g.imag
            local[k] *= factor
            ext[k] *= factor
    return local.reshape(6 * N, N), ext.reshape(6 * N, EXT)


def halves(table):
    table = np.asarray(table, dtype=np.float32)
    high = table.astype(jnp.bfloat16)
    low = (table - high.astype(np.float32)).astype(jnp.bfloat16)
    return np.stack([high, low])


def split(x):
    high = x.astype(jnp.bfloat16)
    return high, (x - high.astype(jnp.float32)).astype(jnp.bfloat16)


def mm(a, b, rhs_lanes=False):
    dims = (((1,), (1 if rhs_lanes else 0,)), ((), ()))

    def one(x, y):
        return lax.dot_general(x, y, dims, preferred_element_type=jnp.float32)

    return one(a[0], b[0]) + (one(a[0], b[1]) + one(a[1], b[0]))


def kernel(
    count,
    x_hbm,
    m_hbm,
    loc_hbm,
    ext_hbm,
    comb_hbm,
    o_hbm,
    x_ref,
    m_ref,
    loc_ref,
    ext_ref,
    cv_ref,
    ch_ref,
    fold_ref,
    pv_ref,
    ph_ref,
    pb_ref,
    gv_ref,
    gh_ref,
    gb_ref,
    tloc_ref,
    acc_ref,
    o_ref,
    in_sems,
    out_sems,
    send_sems,
    recv_sems,
):
    me_r, me_c = lax.axis_index("row"), lax.axis_index("col")
    span = count * 16

    barrier = pltpu.get_barrier_semaphore()
    for d in range(1, count):
        pl.semaphore_signal(barrier, inc=1, device_id=(lax.rem(me_r + d, count), me_c), device_id_type=MESH)
        pl.semaphore_signal(barrier, inc=1, device_id=(me_r, lax.rem(me_c + d, count)), device_id_type=MESH)

    loads = [
        pltpu.make_async_copy(src, dst, in_sems.at[k])
        for k, (src, dst) in enumerate(
            (
                (x_hbm, x_ref),
                (m_hbm, m_ref),
                (comb_hbm.at[me_c], ch_ref),
                (ext_hbm, ext_ref),
                (comb_hbm.at[me_r], cv_ref),
                (loc_hbm, loc_ref),
            )
        )
    ]
    for load in loads:
        load.start()

    loads[0].wait()
    loads[1].wait()
    x = split(x_ref[...])
    m = (m_ref[0], m_ref[1])
    pv = mm(m, x)
    ph = mm(m, x, True)
    pv_ref[...] = pv
    ph_ref[...] = ph
    gv_ref[pl.ds(pl.multiple_of(me_r * 16, 16), 16), :] = pv[:16]
    gh_ref[pl.ds(pl.multiple_of(me_c * 16, 16), 16), :] = ph[:16]

    def message(kind, d, src, dst):
        me = me_r if kind == 0 else me_c
        to = lax.rem(me + d, count)
        off = pl.multiple_of(((me + d) // count) * 8, 8)
        return pltpu.make_async_remote_copy(
            src_ref=src.at[pl.ds(off, 16)],
            dst_ref=dst.at[pl.ds(pl.multiple_of(me * 16, 16), 16)],
            send_sem=send_sems.at[kind, d],
            recv_sem=recv_sems.at[kind, d],
            device_id=(to, me_c) if kind == 0 else (me_r, to),
            device_id_type=MESH,
        )

    order = sorted(range(1, count), key=lambda d: -min(d, count - d))
    down = [message(0, d, pv_ref, gv_ref) for d in order]
    across = [message(1, d, ph_ref, gh_ref) for d in order]

    pl.semaphore_wait(barrier, 2 * (count - 1))
    for copy in down:
        copy.start()
    for copy in across:
        copy.start()

    for k in (2, 3):
        loads[k].wait()
    ext_t = (ext_ref[0], ext_ref[1])
    fold = split(mm(ext_t, (ch_ref[0], ch_ref[1])))
    fold_ref[0], fold_ref[1] = fold
    loads[4].wait()
    loads[5].wait()
    loc_t = (loc_ref[0], loc_ref[1])
    tloc_ref[...] = mm(loc_t, x, True)

    for copy in down:
        copy.wait_recv()
    lines = split(mm((cv_ref[0], cv_ref[1]), split(gv_ref[...])))
    pb = mm(m, lines, True)
    pb = jnp.concatenate([pb, jnp.zeros((24, 128 - EXT), jnp.float32)], axis=1)
    pb_ref[...] = pb
    gb_ref[pl.ds(pl.multiple_of(me_c * 16, 16), 16), :] = pb[:16]
    corner = [message(2, d, pb_ref, gb_ref) for d in order]
    for copy in corner:
        copy.start()

    text = mm(loc_t, lines, True)
    for copy in across:
        copy.wait_recv()
    fold_t = (fold_ref[0], fold_ref[1])
    tloc = tloc_ref[...] + mm(fold_t, split(gh_ref[...]))
    for level in range(2):
        for f, (a, b) in enumerate(FEATURES):
            rows = slice((level * 3 + a) * N, (level * 3 + a + 1) * N)
            cols = slice((level * 3 + b) * N, (level * 3 + b + 1) * N)
            acc_ref[level * 6 + f] = mm((loc_ref[0, rows], loc_ref[1, rows]), split(tloc[cols]), True)

    for copy in corner:
        copy.wait_recv()
    text = text + mm(fold_t, split(gb_ref[...][:, :EXT]))
    outs = []
    for level in range(2):
        for f, (a, b) in enumerate(FEATURES):
            rows = slice((level * 3 + a) * N, (level * 3 + a + 1) * N)
            cols = slice((level * 3 + b) * N, (level * 3 + b + 1) * N)
            k = level * 6 + f
            full = acc_ref[k] + mm((ext_ref[0, rows], ext_ref[1, rows]), split(text[cols]), True)
            o_ref[k] = full.astype(jnp.bfloat16)
            copy = pltpu.make_async_copy(o_ref.at[k], o_hbm.at[k], out_sems.at[k])
            copy.start()
            outs.append(copy)
    for copy in outs:
        copy.wait()
    for copy in down + across + corner:
        copy.wait_send()


def on_device(count, tables, image):
    local, ext, summary, comb = tables
    f32, bf16 = jnp.float32, jnp.bfloat16
    span = count * 16
    return pl.pallas_call(
        functools.partial(kernel, count),
        out_shape=jax.ShapeDtypeStruct((12, N, N), bf16),
        in_specs=[pl.BlockSpec(memory_space=pl.ANY)] * 5,
        out_specs=pl.BlockSpec(memory_space=pl.ANY),
        scratch_shapes=[
            pltpu.VMEM((N, N), f32),
            pltpu.VMEM((2, 24, N), bf16),
            pltpu.VMEM((2, 6 * N, N), bf16),
            pltpu.VMEM((2, 6 * N, EXT), bf16),
            pltpu.VMEM((2, EXT, span), bf16),
            pltpu.VMEM((2, EXT, span), bf16),
            pltpu.VMEM((2, 6 * N, span), bf16),
            pltpu.VMEM((24, N), f32),
            pltpu.VMEM((24, N), f32),
            pltpu.VMEM((24, N), f32),
            pltpu.VMEM((span, N), f32),
            pltpu.VMEM((span, N), f32),
            pltpu.VMEM((span, N), f32),
            pltpu.VMEM((6 * N, N), f32),
            pltpu.VMEM((12, N, N), f32),
            pltpu.VMEM((12, N, N), bf16),
            pltpu.SemaphoreType.DMA((6,)),
            pltpu.SemaphoreType.DMA((12,)),
            pltpu.SemaphoreType.DMA((3, count)),
            pltpu.SemaphoreType.DMA((3, count)),
        ],
        compiler_params=pltpu.CompilerParams(collective_id=0, has_side_effects=True),
    )(image, jnp.asarray(summary), jnp.asarray(local), jnp.asarray(ext), jnp.asarray(comb))


def solution(mesh):
    count = mesh.shape["row"]
    local, ext = filter_tables()
    tables = (
        halves(local),
        halves(ext),
        halves(summary_table()),
        halves(combine_table(count)).swapaxes(0, 1),
    )
    return jax.shard_map(
        functools.partial(on_device, count, tables),
        mesh=mesh,
        in_specs=(P("row", "col"),),
        out_specs=P(None, "row", "col"),
        check_vma=False,
    )
```

```python
import functools
import math

import jax
import jax.numpy as jnp
import numpy as np
from jax import lax
from jax.experimental import pallas as pl
from jax.experimental.pallas import tpu as pltpu
from jax.sharding import PartitionSpec as P

SCALES = (128, 256)
DER_FIRST = (1.0 / 280, -4.0 / 105, 1.0 / 5, -4.0 / 5, 0.0, 4.0 / 5, -1.0 / 5, 4.0 / 105, -1.0 / 280)
DER_SECOND = (-1.0 / 560, 8.0 / 315, -1.0 / 5, 8.0 / 5, -205.0 / 72, 8.0 / 5, -1.0 / 5, 8.0 / 315, -1.0 / 560)
DER_NONE = (0.0, 0.0, 0.0, 0.0, 1.0, 0.0, 0.0, 0.0, 0.0)
DERS = (DER_NONE, DER_FIRST, DER_SECOND)
DERICHE_POLES = ((1.68, 3.735, 1.783, 0.6318), (-0.6803, -0.2598, 1.723, 1.997))
FEATURES = ((0, 0), (0, 1), (1, 0), (0, 2), (1, 1), (2, 0))
N = 128
EXT = 64
MESH = pl.DeviceIdType.MESH


def poles(deviation):
    total = 0.0
    for cw, sw, decay, freq in DERICHE_POLES:
        z = np.exp(complex(-decay, freq) / deviation)
        q = z / (1.0 - z)
        total += cw + 2.0 * (cw * q.real + sw * q.imag)
    return [
        (complex(cw, -sw) / total, np.exp(complex(-decay, freq) / deviation))
        for cw, sw, decay, freq in DERICHE_POLES
    ]


def kernel_values(deviation, offsets):
    offsets = np.abs(np.asarray(offsets, dtype=np.float64))
    return sum((a * z**offsets).real for a, z in poles(deviation))


def summary_table():
    table = np.zeros((24, N))
    n = np.arange(N)
    row = 0
    for s in SCALES:
        for _, z in poles(s):
            causal, anti = z ** (N - 1 - n), z**n
            table[row], table[row + 1] = causal.real, causal.imag
            table[16 + row], table[17 + row] = anti.real, anti.imag
            row += 2
    for k in range(4):
        table[8 + k, k] = 1.0
        table[12 + k, N - 4 + k] = 1.0
    return table


def combine_table(count):
    table = np.zeros((count, EXT, count * 16))
    for pos in range(count):
        w = table[pos]
        for k in range(4):
            if pos > 0:
                w[k, (pos - 1) * 16 + 8 + 4 + k] = 1.0
            if pos < count - 1:
                w[4 + k, (pos + 1) * 16 + k] = 1.0
        for si, s in enumerate(SCALES):
            for ai, der in enumerate(DERS):
                for pi, (_, z) in enumerate(poles(s)):
                    up = 8 + (si * 3 + ai) * 8 + pi * 2
                    down = up + 4
                    col = si * 4 + pi * 2
                    dz = sum(der[t + 4] * z**t for t in range(-4, 5))
                    dinv = sum(der[t + 4] * z ** (-t) for t in range(-4, 5))
                    for src in range(count):
                        if src < pos:
                            g = dz * z ** (N * (pos - 1 - src))
                            at = src * 16 + col
                            w[up, at], w[up, at + 1] = g.real, -g.imag
                            w[up + 1, at], w[up + 1, at + 1] = g.imag, g.real
                        if src > pos:
                            g = dinv * z ** (N * (src - pos - 1))
                            at = src * 16 + 8 + col
                            w[down, at], w[down, at + 1] = g.real, -g.imag
                            w[down + 1, at], w[down + 1, at + 1] = g.imag, g.real
                    first = 8
                    last = (count - 1) * 16 + (8 + 4 if pos == count - 1 else 4)
                    for n in range(4):
                        g = -sum(
                            der[n - m + 4] * z ** (N * pos - 1 - m)
                            for m in range(-4, 0)
                            if -4 <= n - m <= 4
                        )
                        w[up, first + n] += g.real
                        w[up + 1, first + n] += g.imag
                        g = -sum(
                            der[n - 4 - m + 4] * z ** (N * (count - 1 - pos) + m)
                            for m in range(0, 4)
                            if -4 <= n - 4 - m <= 4
                        )
                        w[down, last + n] += g.real
                        w[down + 1, last + n] += g.imag
    return table


def filter_tables():
    local = np.zeros((6, N, N))
    ext = np.zeros((6, N, EXT))
    c = np.arange(N)
    for si, s in enumerate(SCALES):
        base = 2.0 * math.sqrt(math.pi) * s
        for ai, der in enumerate(DERS):
            k = si * 3 + ai
            factor = math.sqrt(base) * float(s) ** ai

            def kappa(d):
                return sum(der[t + 4] * kernel_values(s, d + t) for t in range(-4, 5))

            local[k] = kappa(c[:, None] - c[None, :])
            for n in range(4):
                up, down = n - 4, N + n
                ext[k, :, n] = kappa(c - up)
                ext[k, :, 4 + n] = kappa(c - down)
                for a, z in poles(s):
                    dz = sum(der[t + 4] * z**t for t in range(-4, 5))
                    dinv = sum(der[t + 4] * z ** (-t) for t in range(-4, 5))
                    ext[k, :, n] -= (a * dz * z ** (c - up + 0.0)).real
                    ext[k, :, 4 + n] -= (a * dinv * z ** (down - c + 0.0)).real
                ext[k, 4:, n] = 0.0
                ext[k, : N - 4, 4 + n] = 0.0
            for pi, (a, z) in enumerate(poles(s)):
                up = 8 + k * 8 + pi * 2
                g = a * z ** (c + 1.0)
                ext[k, :, up], ext[k, :, up + 1] = g.real, -g.imag
                g = a * z ** (N - c + 0.0)
                ext[k, :, up + 4], ext[k, :, up + 5] = g.real, -g.imag
            local[k] *= factor
            ext[k] *= factor
    return local.reshape(6 * N, N), ext.reshape(6 * N, EXT)


def halves(table):
    table = np.asarray(table, dtype=np.float32)
    high = table.astype(jnp.bfloat16)
    low = (table - high.astype(np.float32)).astype(jnp.bfloat16)
    return high, low


def packed_table(count):
    local, ext = (halves(t) for t in filter_tables())
    summary = halves(np.pad(summary_table(), ((0, 8), (0, 0))))
    comb = halves(combine_table(count))
    return np.concatenate(
        [
            np.concatenate(summary, axis=1),
            np.concatenate(local, axis=1),
            np.concatenate([ext[0], ext[0], ext[1], ext[1]], axis=1),
            np.concatenate(comb, axis=1).reshape(count * 2 * EXT, count * 16),
        ]
    )


LOC_AT, EXT_AT, COMB_AT = 32, 32 + 6 * N, 32 + 12 * N


def split(x):
    high = x.astype(jnp.bfloat16)
    return high, (x - high.astype(jnp.float32)).astype(jnp.bfloat16)


def dot(a, b, rhs_lanes=False):
    dims = (((1,), (1 if rhs_lanes else 0,)), ((), ()))
    return lax.dot_general(a, b, dims, preferred_element_type=jnp.float32)


def mm(a, b, rhs_lanes=False):
    return dot(a[0], b[0], rhs_lanes) + (dot(a[0], b[1], rhs_lanes) + dot(a[1], b[0], rhs_lanes))


def kernel(
    count,
    x_hbm,
    tab_hbm,
    o_ref,
    x_ref,
    m_ref,
    loc_ref,
    ext_ref,
    cv_ref,
    ch_ref,
    pv_ref,
    ph_ref,
    pb_ref,
    gv_ref,
    gh_ref,
    gb_ref,
    acc_ref,
    in_sems,
    send_sems,
    recv_sems,
    late_sem,
    row_sem,
    ok_sems,
):
    me_r, me_c = lax.axis_index("row"), lax.axis_index("col")
    part = count // 2
    half, spot = me_c // part, lax.rem(me_c, part)
    span = count * 16

    def load(k, src, dst):
        return pltpu.make_async_copy(src, dst, in_sems.at[k])

    def comb_at(pos):
        return tab_hbm.at[pl.ds(pl.multiple_of(COMB_AT + pos * 2 * EXT, 16), 2 * EXT)]

    loads = [
        load(0, x_hbm, x_ref),
        load(1, tab_hbm.at[pl.ds(0, 32)], m_ref),
        load(2, comb_at(me_r), cv_ref),
        load(3, tab_hbm.at[pl.ds(LOC_AT, 6 * N)], loc_ref),
        load(4, tab_hbm.at[pl.ds(EXT_AT, 6 * N)], ext_ref),
        load(5, comb_at(me_c), ch_ref),
    ]
    for copy in loads:
        copy.start()

    def near(d):
        return half * part + lax.rem(spot + d, part)

    def far(d):
        return (1 - half) * part + lax.rem(spot + d, part)

    barrier = pltpu.get_barrier_semaphore()

    def greet(sem, row, col):
        pl.semaphore_signal(sem, inc=1, device_id=(row, col), device_id_type=MESH)

    @pl.when(half == 0)
    def _():
        for d in range(part):
            greet(barrier, me_r, far(d))
        for d in range(1, part):
            greet(barrier, me_r, near(d))
        for d in range(1, count):
            greet(barrier, lax.rem(me_r + d, count), me_c)

    @pl.when(half == 1)
    def _():
        pl.semaphore_wait(barrier, part)
        for d in range(part):
            greet(late_sem, me_r, far(d))

    def message(kind, k, to, src, dst):
        me = me_c if kind == 0 else me_r
        off = pl.multiple_of(((me - to + count - 1) // count) * 8, 8)
        return pltpu.make_async_remote_copy(
            src_ref=src.at[pl.ds(off, 16)],
            dst_ref=dst.at[pl.ds(pl.multiple_of(me * 16, 16), 16)],
            send_sem=send_sems.at[kind, k],
            recv_sem=recv_sems.at[kind, k],
            device_id=(me_r, to) if kind == 0 else (to, me_c),
            device_id_type=MESH,
        )

    across_near = [message(0, d, near(d), ph_ref, gh_ref) for d in range(1, part)]
    across_far = [message(0, part + d, far(d), ph_ref, gh_ref) for d in range(part)]
    order = sorted(range(1, count), key=lambda d: -min(d, count - d))
    down = [message(1, d, lax.rem(me_r + d, count), pv_ref, gv_ref) for d in order]
    corner = [message(2, d, lax.rem(me_r + d, count), pb_ref, gb_ref) for d in order]

    loads[0].wait()
    loads[1].wait()
    x = split(x_ref[...])
    m = (m_ref[:24, :N], m_ref[:24, N:])
    ph = mm(m, x, True)
    ph_ref[...] = ph
    gh_ref[pl.ds(pl.multiple_of(me_c * 16, 16), 16), :] = ph[:16]
    pv = mm(m, x)
    pv_ref[...] = pv
    gv_ref[pl.ds(pl.multiple_of(me_r * 16, 16), 16), :] = pv[:16]

    mirror = count - 2 - me_c // 2 * 2 + lax.rem(me_c, 2)

    @pl.when(half == 0)
    def _():
        pl.semaphore_wait(barrier, count - 1 + part - 1)
        for copy in across_near:
            copy.start()
        for copy in down:
            copy.start()
        pl.semaphore_wait(late_sem, part)
        greet(ok_sems.at[0], me_r, mirror)
        for d in range(1, count):
            greet(row_sem, lax.rem(me_r + d, count), me_c)
        for copy in across_far:
            copy.start()
        pl.semaphore_wait(row_sem, count - 1)
        greet(ok_sems.at[1], me_r, mirror)

    @pl.when(half == 1)
    def _():
        for copy in across_far:
            copy.start()
        pl.semaphore_wait(ok_sems.at[0], 1)
        for copy in across_near:
            copy.start()
        pl.semaphore_wait(ok_sems.at[1], 1)
        for copy in down:
            copy.start()

    def stacked(v):
        return jnp.concatenate([v[0], v[1], v[0], v[1]], axis=0)

    def combine(c_ref, g_ref):
        return mm((c_ref[:EXT], c_ref[EXT:]), split(g_ref[...]))

    loads[5].wait()
    for copy in across_near + across_far:
        copy.wait_recv()
    lines = combine(ch_ref, gh_ref)
    lines = split(jnp.concatenate([lines, lines], axis=0))
    pb = mm(m, lines, True)
    pb_ref[...] = pb
    gb_ref[pl.ds(pl.multiple_of(me_r * 16, 16), 16), :] = pb[:16]
    for copy in corner:
        copy.start()
    for k in (2, 3, 4):
        loads[k].wait()
    filtered = dot(loc_ref[...], jnp.concatenate([x[0], x[0]], axis=0)) + dot(loc_ref[:, :N], x[1])
    for copy in down:
        copy.wait_recv()
    filtered = filtered + dot(ext_ref[...], stacked(split(combine(cv_ref, gv_ref))))
    for level in range(2):
        for a in range(3):
            k = level * 3 + a
            wide = slice(level * 3 * N, (level * 3 + 3 - a) * N)
            t = split(filtered[k * N : (k + 1) * N])
            acc_ref[k, :, : (3 - a) * N] = dot(
                jnp.concatenate([t[0], t[0]], axis=1), loc_ref[wide], True
            ) + dot(t[1], loc_ref[wide, :N], True)

    carried = mm((loc_ref[:, :N], loc_ref[:, N:]), lines, True)
    for copy in corner:
        copy.wait_recv()
    carried = carried + dot(ext_ref[...], stacked(split(combine(cv_ref, gb_ref))))

    high = carried.astype(jnp.bfloat16).astype(jnp.float32)
    lane = lax.broadcasted_iota(jnp.int32, carried.shape, 1)
    pair = jnp.where(lane < EXT, high, carried - high).astype(jnp.bfloat16)
    pair = jnp.concatenate([pair, pair], axis=1)
    for level in range(2):
        for a in range(3):
            k = level * 3 + a
            wide = slice(level * 3 * N, (level * 3 + 3 - a) * N)
            full = acc_ref[k, :, : (3 - a) * N] + dot(pair[k * N : (k + 1) * N], ext_ref[wide], True)
            for b in range(3 - a):
                f = FEATURES.index((a, b))
                o_ref[level * 6 + f] = full[:, b * N : (b + 1) * N].astype(jnp.bfloat16)
    for copy in across_near + across_far + down + corner:
        copy.wait_send()


def on_device(count, table, image):
    f32, bf16 = jnp.float32, jnp.bfloat16
    span = count * 16
    return pl.pallas_call(
        functools.partial(kernel, count),
        out_shape=jax.ShapeDtypeStruct((12, N, N), bf16),
        in_specs=[pl.BlockSpec(memory_space=pl.ANY)] * 2,
        out_specs=pl.BlockSpec(memory_space=pltpu.VMEM),
        scratch_shapes=[
            pltpu.VMEM((N, N), f32),
            pltpu.VMEM((32, 256), bf16),
            pltpu.VMEM((6 * N, 256), bf16),
            pltpu.VMEM((6 * N, 256), bf16),
            pltpu.VMEM((2 * EXT, span), bf16),
            pltpu.VMEM((2 * EXT, span), bf16),
            pltpu.VMEM((24, N), f32),
            pltpu.VMEM((24, N), f32),
            pltpu.VMEM((24, N), f32),
            pltpu.VMEM((span, N), f32),
            pltpu.VMEM((span, N), f32),
            pltpu.VMEM((span, N), f32),
            pltpu.VMEM((6, N, 3 * N), f32),
            pltpu.SemaphoreType.DMA((6,)),
            pltpu.SemaphoreType.DMA((3, count)),
            pltpu.SemaphoreType.DMA((3, count)),
            pltpu.SemaphoreType.REGULAR,
            pltpu.SemaphoreType.REGULAR,
            pltpu.SemaphoreType.REGULAR((2,)),
        ],
        compiler_params=pltpu.CompilerParams(
            collective_id=0, has_side_effects=True, vmem_limit_bytes=VMEM_LIMIT
        ),
    )(image, jnp.asarray(table))


VMEM_LIMIT = 54000 << 10


def solution(mesh):
    count = mesh.shape["row"]
    return jax.shard_map(
        functools.partial(on_device, count, packed_table(count)),
        mesh=mesh,
        in_specs=(P("row", "col"),),
        out_specs=P(None, "row", "col"),
        check_vma=False,
    )
```

```python
import functools
import math

import jax
import jax.numpy as jnp
import numpy as np
from jax import lax
from jax.experimental import pallas as pl
from jax.experimental.pallas import tpu as pltpu
from jax.sharding import PartitionSpec as P

SCALES = (128, 256)
DER_FIRST = (1.0 / 280, -4.0 / 105, 1.0 / 5, -4.0 / 5, 0.0, 4.0 / 5, -1.0 / 5, 4.0 / 105, -1.0 / 280)
DER_SECOND = (-1.0 / 560, 8.0 / 315, -1.0 / 5, 8.0 / 5, -205.0 / 72, 8.0 / 5, -1.0 / 5, 8.0 / 315, -1.0 / 560)
DER_NONE = (0.0, 0.0, 0.0, 0.0, 1.0, 0.0, 0.0, 0.0, 0.0)
DERS = (DER_NONE, DER_FIRST, DER_SECOND)
DERICHE_POLES = ((1.68, 3.735, 1.783, 0.6318), (-0.6803, -0.2598, 1.723, 1.997))
FEATURES = ((0, 0), (0, 1), (1, 0), (0, 2), (1, 1), (2, 0))
N = 128
EXT = 64
MESH = pl.DeviceIdType.MESH


def poles(deviation):
    total = 0.0
    for cw, sw, decay, freq in DERICHE_POLES:
        z = np.exp(complex(-decay, freq) / deviation)
        q = z / (1.0 - z)
        total += cw + 2.0 * (cw * q.real + sw * q.imag)
    return [
        (complex(cw, -sw) / total, np.exp(complex(-decay, freq) / deviation))
        for cw, sw, decay, freq in DERICHE_POLES
    ]


def kernel_values(deviation, offsets):
    offsets = np.abs(np.asarray(offsets, dtype=np.float64))
    return sum((a * z**offsets).real for a, z in poles(deviation))


def summary_table():
    table = np.zeros((24, N))
    n = np.arange(N)
    row = 0
    for s in SCALES:
        for _, z in poles(s):
            causal, anti = z ** (N - 1 - n), z**n
            table[row], table[row + 1] = causal.real, causal.imag
            table[16 + row], table[17 + row] = anti.real, anti.imag
            row += 2
    for k in range(4):
        table[8 + k, k] = 1.0
        table[12 + k, N - 4 + k] = 1.0
    return table


def combine_table(count):
    table = np.zeros((count, EXT, count * 16))
    for pos in range(count):
        w = table[pos]
        for k in range(4):
            if pos > 0:
                w[k, (pos - 1) * 16 + 8 + 4 + k] = 1.0
            if pos < count - 1:
                w[4 + k, (pos + 1) * 16 + k] = 1.0
        for si, s in enumerate(SCALES):
            for ai, der in enumerate(DERS):
                for pi, (_, z) in enumerate(poles(s)):
                    up = 8 + (si * 3 + ai) * 8 + pi * 2
                    down = up + 4
                    col = si * 4 + pi * 2
                    dz = sum(der[t + 4] * z**t for t in range(-4, 5))
                    dinv = sum(der[t + 4] * z ** (-t) for t in range(-4, 5))
                    for src in range(count):
                        if src < pos:
                            g = dz * z ** (N * (pos - 1 - src))
                            at = src * 16 + col
                            w[up, at], w[up, at + 1] = g.real, -g.imag
                            w[up + 1, at], w[up + 1, at + 1] = g.imag, g.real
                        if src > pos:
                            g = dinv * z ** (N * (src - pos - 1))
                            at = src * 16 + 8 + col
                            w[down, at], w[down, at + 1] = g.real, -g.imag
                            w[down + 1, at], w[down + 1, at + 1] = g.imag, g.real
                    first = 8
                    last = (count - 1) * 16 + (8 + 4 if pos == count - 1 else 4)
                    for n in range(4):
                        g = -sum(
                            der[n - m + 4] * z ** (N * pos - 1 - m)
                            for m in range(-4, 0)
                            if -4 <= n - m <= 4
                        )
                        w[up, first + n] += g.real
                        w[up + 1, first + n] += g.imag
                        g = -sum(
                            der[n - 4 - m + 4] * z ** (N * (count - 1 - pos) + m)
                            for m in range(0, 4)
                            if -4 <= n - 4 - m <= 4
                        )
                        w[down, last + n] += g.real
                        w[down + 1, last + n] += g.imag
    return table


def filter_tables():
    local = np.zeros((6, N, N))
    ext = np.zeros((6, N, EXT))
    c = np.arange(N)
    for si, s in enumerate(SCALES):
        base = 2.0 * math.sqrt(math.pi) * s
        for ai, der in enumerate(DERS):
            k = si * 3 + ai
            factor = math.sqrt(base) * float(s) ** ai

            def kappa(d):
                return sum(der[t + 4] * kernel_values(s, d + t) for t in range(-4, 5))

            local[k] = kappa(c[:, None] - c[None, :])
            for n in range(4):
                up, down = n - 4, N + n
                ext[k, :, n] = kappa(c - up)
                ext[k, :, 4 + n] = kappa(c - down)
                for a, z in poles(s):
                    dz = sum(der[t + 4] * z**t for t in range(-4, 5))
                    dinv = sum(der[t + 4] * z ** (-t) for t in range(-4, 5))
                    ext[k, :, n] -= (a * dz * z ** (c - up + 0.0)).real
                    ext[k, :, 4 + n] -= (a * dinv * z ** (down - c + 0.0)).real
                ext[k, 4:, n] = 0.0
                ext[k, : N - 4, 4 + n] = 0.0
            for pi, (a, z) in enumerate(poles(s)):
                up = 8 + k * 8 + pi * 2
                g = a * z ** (c + 1.0)
                ext[k, :, up], ext[k, :, up + 1] = g.real, -g.imag
                g = a * z ** (N - c + 0.0)
                ext[k, :, up + 4], ext[k, :, up + 5] = g.real, -g.imag
            local[k] *= factor
            ext[k] *= factor
    return local.reshape(6 * N, N), ext.reshape(6 * N, EXT)


def halves(table):
    table = np.asarray(table, dtype=np.float32)
    high = table.astype(jnp.bfloat16)
    low = (table - high.astype(np.float32)).astype(jnp.bfloat16)
    return high, low


def packed_table(count):
    local, ext = (halves(t) for t in filter_tables())
    comb = halves(combine_table(count))
    return np.concatenate(
        [
            np.concatenate(local, axis=1),
            np.concatenate([ext[0], ext[0], ext[1], ext[1]], axis=1),
            np.concatenate(comb, axis=1).reshape(count * 2 * EXT, count * 16),
        ]
    )


LOC_AT, EXT_AT, COMB_AT = 0, 6 * N, 12 * N


def split(x):
    high = x.astype(jnp.bfloat16)
    return high, (x - high.astype(jnp.float32)).astype(jnp.bfloat16)


def dot(a, b, rhs_lanes=False):
    dims = (((1,), (1 if rhs_lanes else 0,)), ((), ()))
    return lax.dot_general(a, b, dims, preferred_element_type=jnp.float32)


def mm(a, b, rhs_lanes=False):
    return dot(a[0], b[0], rhs_lanes) + (dot(a[0], b[1], rhs_lanes) + dot(a[1], b[0], rhs_lanes))


def summary_lines():
    shape = (24, N)
    row = lax.broadcasted_iota(jnp.int32, shape, 0)
    n = lax.broadcasted_iota(jnp.int32, shape, 1)
    part = lax.rem(row, 8)
    pairs = [(d / s, f / s) for s in SCALES for _, _, d, f in DERICHE_POLES]
    rate, freq = (
        jnp.where(
            part < 4,
            jnp.where(part < 2, pairs[0][i], pairs[1][i]),
            jnp.where(part < 6, pairs[2][i], pairs[3][i]),
        )
        for i in range(2)
    )
    steps = jnp.where(row < 8, N - 1 - n, n).astype(jnp.float32)
    angle = freq * steps - jnp.where(lax.rem(row, 2) == 1, math.pi / 2, 0.0)
    square = angle * angle
    cosine = jnp.full(shape, 1.0 / math.factorial(18), jnp.float32)
    for k in range(8, -1, -1):
        cosine = 1.0 / math.factorial(2 * k) - cosine * square
    wave = jnp.exp(-rate * steps) * cosine
    cell = jnp.where(row < 12, row - 8, row + N - 16)
    pick = jnp.where(n == cell, 1.0, 0.0)
    return jnp.where((row >= 8) & (row < 16), pick, wave)


def kernel(
    count,
    x_hbm,
    tab_hbm,
    o_ref,
    x_ref,
    loc_ref,
    ext_ref,
    cv_ref,
    ch_ref,
    pv_ref,
    ph_ref,
    pb_ref,
    gv_ref,
    gh_ref,
    gb_ref,
    acc_ref,
    in_sems,
    send_sems,
    recv_sems,
    late_sem,
    mirror_sem,
    near_sem,
    row_sem,
    ok_sem,
):
    me_r, me_c = lax.axis_index("row"), lax.axis_index("col")
    part = count // 2
    half, spot = me_c // part, lax.rem(me_c, part)
    span = count * 16

    def load(k, src, dst):
        return pltpu.make_async_copy(src, dst, in_sems.at[k])

    def comb_at(pos):
        return tab_hbm.at[pl.ds(pl.multiple_of(COMB_AT + pos * 2 * EXT, 16), 2 * EXT)]

    image, *loads = [
        load(4, x_hbm, x_ref),
        load(0, comb_at(me_c), ch_ref),
        load(1, comb_at(me_r), cv_ref),
        load(2, tab_hbm.at[pl.ds(LOC_AT, 6 * N)], loc_ref),
        load(3, tab_hbm.at[pl.ds(EXT_AT, 6 * N)], ext_ref),
    ]
    image.start()
    for copy in loads:
        copy.start()

    def near(d):
        return half * part + lax.rem(spot + d, part)

    def far(d):
        return (1 - half) * part + lax.rem(spot + d, part)

    barrier = pltpu.get_barrier_semaphore()

    def greet(sem, row, col):
        pl.semaphore_signal(sem, inc=1, device_id=(row, col), device_id_type=MESH)

    @pl.when(half == 0)
    def _():
        for d in range(part):
            greet(barrier, me_r, far(d))
        for d in range(1, part):
            greet(barrier, me_r, near(d))
        for d in range(1, count):
            greet(barrier, lax.rem(me_r + d, count), me_c)

    mirror = count - 2 - me_c // 2 * 2 + lax.rem(me_c, 2)

    @pl.when(half == 1)
    def _():
        pl.semaphore_wait(barrier, part)
        greet(mirror_sem, me_r, mirror)
        for d in range(part):
            greet(late_sem, me_r, far(d))

    def message(kind, k, to, src, dst):
        me = me_c if kind == 0 else me_r
        off = pl.multiple_of(((me - to + count - 1) // count) * 8, 8)
        return pltpu.make_async_remote_copy(
            src_ref=src.at[pl.ds(off, 16)],
            dst_ref=dst.at[pl.ds(pl.multiple_of(me * 16, 16), 16)],
            send_sem=send_sems.at[kind, k],
            recv_sem=recv_sems.at[kind, k],
            device_id=(me_r, to) if kind == 0 else (to, me_c),
            device_id_type=MESH,
        )

    order = sorted(range(1, count), key=lambda d: -min(d, count - d))

    def send_near():
        for d in range(1, part):
            message(0, d, near(d), ph_ref, gh_ref).start()

    def send_far():
        for d in range(part):
            message(0, part + d, far(d), ph_ref, gh_ref).start()

    def send_rows(kind, src, dst):
        for d in order:
            message(kind, d, lax.rem(me_r + d, count), src, dst).start()

    def received(kind, dst):
        for d in range(1, count):
            pltpu.make_async_copy(dst.at[:16], dst.at[:16], recv_sems.at[kind, d]).wait()

    image.wait()
    x = split(x_ref[...])
    m = split(summary_lines())
    ph = mm(m, x, True)
    ph_ref[...] = ph
    gh_ref[pl.ds(pl.multiple_of(me_c * 16, 16), 16), :] = ph[:16]
    pv = mm(m, x)
    pv_ref[...] = pv
    gv_ref[pl.ds(pl.multiple_of(me_r * 16, 16), 16), :] = pv[:16]

    @pl.when(half == 0)
    def _():
        pl.semaphore_wait(barrier, count - 1 + part - 1)
        send_near()
        send_rows(1, pv_ref, gv_ref)
        pl.semaphore_wait(mirror_sem, 1)
        for d in range(1, count):
            greet(row_sem, lax.rem(me_r + d, count), me_c)
        pl.semaphore_wait(late_sem, part)
        greet(near_sem, me_r, mirror)
        send_far()
        pl.semaphore_wait(row_sem, count - 1)
        greet(ok_sem, me_r, mirror)

    @pl.when(half == 1)
    def _():
        send_far()
        pl.semaphore_wait(near_sem, 1)
        send_near()
        pl.semaphore_wait(ok_sem, 1)
        send_rows(1, pv_ref, gv_ref)

    def stacked(v):
        return jnp.concatenate([v[0], v[1], v[0], v[1]], axis=0)

    def combine(c_ref, g_ref):
        return mm((c_ref[:EXT], c_ref[EXT:]), split(g_ref[...]))

    loads[0].wait()
    received(0, gh_ref)
    lines = combine(ch_ref, gh_ref)
    lines = split(jnp.concatenate([lines, lines], axis=0))
    pb = mm(m, lines, True)
    pb_ref[...] = pb
    gb_ref[pl.ds(pl.multiple_of(me_r * 16, 16), 16), :] = pb[:16]
    send_rows(2, pb_ref, gb_ref)
    for k in (1, 2, 3):
        loads[k].wait()
    filtered = dot(loc_ref[...], jnp.concatenate([x[0], x[0]], axis=0)) + dot(loc_ref[:, :N], x[1])
    received(1, gv_ref)
    filtered = filtered + dot(ext_ref[...], stacked(split(combine(cv_ref, gv_ref))))
    for level in range(2):
        for a in range(3):
            k = level * 3 + a
            wide = slice(level * 3 * N, (level * 3 + 3 - a) * N)
            t = split(filtered[k * N : (k + 1) * N])
            acc_ref[k, :, : (3 - a) * N] = dot(
                jnp.concatenate([t[0], t[0]], axis=1), loc_ref[wide], True
            ) + dot(t[1], loc_ref[wide, :N], True)

    carried = mm((loc_ref[:, :N], loc_ref[:, N:]), lines, True)
    received(2, gb_ref)
    carried = carried + dot(ext_ref[...], stacked(split(combine(cv_ref, gb_ref))))

    high = carried.astype(jnp.bfloat16).astype(jnp.float32)
    lane = lax.broadcasted_iota(jnp.int32, carried.shape, 1)
    pair = jnp.where(lane < EXT, high, carried - high).astype(jnp.bfloat16)
    pair = jnp.concatenate([pair, pair], axis=1)
    for level in range(2):
        for a in range(3):
            k = level * 3 + a
            wide = slice(level * 3 * N, (level * 3 + 3 - a) * N)
            full = acc_ref[k, :, : (3 - a) * N] + dot(pair[k * N : (k + 1) * N], ext_ref[wide], True)
            for b in range(3 - a):
                f = FEATURES.index((a, b))
                o_ref[level * 6 + f] = full[:, b * N : (b + 1) * N].astype(jnp.bfloat16)
    for kind, src in enumerate((ph_ref, pv_ref, pb_ref)):
        for d in range(1, count):
            pltpu.make_async_copy(src.at[:16], src.at[:16], send_sems.at[kind, d]).wait()


def on_device(count, table, image):
    f32, bf16 = jnp.float32, jnp.bfloat16
    span = count * 16
    return pl.pallas_call(
        functools.partial(kernel, count),
        out_shape=jax.ShapeDtypeStruct((12, N, N), bf16),
        in_specs=[pl.BlockSpec(memory_space=pltpu.HBM), pl.BlockSpec(memory_space=pl.ANY)],
        out_specs=pl.BlockSpec(memory_space=pltpu.VMEM),
        scratch_shapes=[
            pltpu.VMEM((N, N), f32),
            pltpu.VMEM((6 * N, 256), bf16),
            pltpu.VMEM((6 * N, 256), bf16),
            pltpu.VMEM((2 * EXT, span), bf16),
            pltpu.VMEM((2 * EXT, span), bf16),
            pltpu.VMEM((24, N), f32),
            pltpu.VMEM((24, N), f32),
            pltpu.VMEM((24, N), f32),
            pltpu.VMEM((span, N), f32),
            pltpu.VMEM((span, N), f32),
            pltpu.VMEM((span, N), f32),
            pltpu.VMEM((6, N, 3 * N), f32),
            pltpu.SemaphoreType.DMA((5,)),
            pltpu.SemaphoreType.DMA((3, count)),
            pltpu.SemaphoreType.DMA((3, count)),
            pltpu.SemaphoreType.REGULAR,
            pltpu.SemaphoreType.REGULAR,
            pltpu.SemaphoreType.REGULAR,
            pltpu.SemaphoreType.REGULAR,
            pltpu.SemaphoreType.REGULAR,
        ],
        compiler_params=pltpu.CompilerParams(
            collective_id=0, has_side_effects=True, vmem_limit_bytes=VMEM_LIMIT
        ),
    )(pltpu.with_memory_space_constraint(image, pltpu.HBM), jnp.asarray(table))


VMEM_LIMIT = 54000 << 10


def solution(mesh):
    count = mesh.shape["row"]
    return jax.shard_map(
        functools.partial(on_device, count, packed_table(count)),
        mesh=mesh,
        in_specs=(P("row", "col"),),
        out_specs=P(None, "row", "col"),
        check_vma=False,
    )
```

```python
import functools
import math

import jax
import jax.numpy as jnp
import numpy as np
from jax import lax
from jax.experimental import pallas as pl
from jax.experimental.pallas import tpu as pltpu
from jax.sharding import PartitionSpec as P

SCALES = (128, 256)
DER_FIRST = (1.0 / 280, -4.0 / 105, 1.0 / 5, -4.0 / 5, 0.0, 4.0 / 5, -1.0 / 5, 4.0 / 105, -1.0 / 280)
DER_SECOND = (-1.0 / 560, 8.0 / 315, -1.0 / 5, 8.0 / 5, -205.0 / 72, 8.0 / 5, -1.0 / 5, 8.0 / 315, -1.0 / 560)
DER_NONE = (0.0, 0.0, 0.0, 0.0, 1.0, 0.0, 0.0, 0.0, 0.0)
DERS = (DER_NONE, DER_FIRST, DER_SECOND)
DERICHE_POLES = ((1.68, 3.735, 1.783, 0.6318), (-0.6803, -0.2598, 1.723, 1.997))
FEATURES = ((0, 0), (0, 1), (1, 0), (0, 2), (1, 1), (2, 0))
N = 128
EXT = 64
MESH = pl.DeviceIdType.MESH


def poles(deviation):
    total = 0.0
    for cw, sw, decay, freq in DERICHE_POLES:
        z = np.exp(complex(-decay, freq) / deviation)
        q = z / (1.0 - z)
        total += cw + 2.0 * (cw * q.real + sw * q.imag)
    return [
        (complex(cw, -sw) / total, np.exp(complex(-decay, freq) / deviation))
        for cw, sw, decay, freq in DERICHE_POLES
    ]


def kernel_values(deviation, offsets):
    offsets = np.abs(np.asarray(offsets, dtype=np.float64))
    return sum((a * z**offsets).real for a, z in poles(deviation))


def summary_table():
    table = np.zeros((24, N))
    n = np.arange(N)
    row = 0
    for s in SCALES:
        for _, z in poles(s):
            causal, anti = z ** (N - 1 - n), z**n
            table[row], table[row + 1] = causal.real, causal.imag
            table[16 + row], table[17 + row] = anti.real, anti.imag
            row += 2
    for k in range(4):
        table[8 + k, k] = 1.0
        table[12 + k, N - 4 + k] = 1.0
    return table


def combine_table(count):
    table = np.zeros((count, EXT, count * 16))
    for pos in range(count):
        w = table[pos]
        for k in range(4):
            if pos > 0:
                w[k, (pos - 1) * 16 + 8 + 4 + k] = 1.0
            if pos < count - 1:
                w[4 + k, (pos + 1) * 16 + k] = 1.0
        for si, s in enumerate(SCALES):
            for ai, der in enumerate(DERS):
                for pi, (_, z) in enumerate(poles(s)):
                    up = 8 + (si * 3 + ai) * 8 + pi * 2
                    down = up + 4
                    col = si * 4 + pi * 2
                    dz = sum(der[t + 4] * z**t for t in range(-4, 5))
                    dinv = sum(der[t + 4] * z ** (-t) for t in range(-4, 5))
                    for src in range(count):
                        if src < pos:
                            g = dz * z ** (N * (pos - 1 - src))
                            at = src * 16 + col
                            w[up, at], w[up, at + 1] = g.real, -g.imag
                            w[up + 1, at], w[up + 1, at + 1] = g.imag, g.real
                        if src > pos:
                            g = dinv * z ** (N * (src - pos - 1))
                            at = src * 16 + 8 + col
                            w[down, at], w[down, at + 1] = g.real, -g.imag
                            w[down + 1, at], w[down + 1, at + 1] = g.imag, g.real
                    first = 8
                    last = (count - 1) * 16 + (8 + 4 if pos == count - 1 else 4)
                    for n in range(4):
                        g = -sum(
                            der[n - m + 4] * z ** (N * pos - 1 - m)
                            for m in range(-4, 0)
                            if -4 <= n - m <= 4
                        )
                        w[up, first + n] += g.real
                        w[up + 1, first + n] += g.imag
                        g = -sum(
                            der[n - 4 - m + 4] * z ** (N * (count - 1 - pos) + m)
                            for m in range(0, 4)
                            if -4 <= n - 4 - m <= 4
                        )
                        w[down, last + n] += g.real
                        w[down + 1, last + n] += g.imag
    return table


def filter_tables():
    local = np.zeros((6, N, N))
    ext = np.zeros((6, N, EXT))
    c = np.arange(N)
    for si, s in enumerate(SCALES):
        base = 2.0 * math.sqrt(math.pi) * s
        for ai, der in enumerate(DERS):
            k = si * 3 + ai
            factor = math.sqrt(base) * float(s) ** ai

            def kappa(d):
                return sum(der[t + 4] * kernel_values(s, d + t) for t in range(-4, 5))

            local[k] = kappa(c[:, None] - c[None, :])
            for n in range(4):
                up, down = n - 4, N + n
                ext[k, :, n] = kappa(c - up)
                ext[k, :, 4 + n] = kappa(c - down)
                for a, z in poles(s):
                    dz = sum(der[t + 4] * z**t for t in range(-4, 5))
                    dinv = sum(der[t + 4] * z ** (-t) for t in range(-4, 5))
                    ext[k, :, n] -= (a * dz * z ** (c - up + 0.0)).real
                    ext[k, :, 4 + n] -= (a * dinv * z ** (down - c + 0.0)).real
                ext[k, 4:, n] = 0.0
                ext[k, : N - 4, 4 + n] = 0.0
            for pi, (a, z) in enumerate(poles(s)):
                up = 8 + k * 8 + pi * 2
                g = a * z ** (c + 1.0)
                ext[k, :, up], ext[k, :, up + 1] = g.real, -g.imag
                g = a * z ** (N - c + 0.0)
                ext[k, :, up + 4], ext[k, :, up + 5] = g.real, -g.imag
            local[k] *= factor
            ext[k] *= factor
    return local.reshape(6 * N, N), ext.reshape(6 * N, EXT)


def halves(table):
    table = np.asarray(table, dtype=np.float32)
    high = table.astype(jnp.bfloat16)
    low = (table - high.astype(np.float32)).astype(jnp.bfloat16)
    return high, low


def packed_table(count):
    local, ext = (halves(t) for t in filter_tables())
    comb = halves(combine_table(count))
    return np.concatenate(
        [
            np.concatenate(local, axis=1),
            np.concatenate([ext[0], ext[0], ext[1], ext[1]], axis=1),
            np.concatenate(comb, axis=1).reshape(count * 2 * EXT, count * 16),
        ]
    )


LOC_AT, EXT_AT, COMB_AT = 0, 6 * N, 12 * N


def split(x):
    high = x.astype(jnp.bfloat16)
    return high, (x - high.astype(jnp.float32)).astype(jnp.bfloat16)


def dot(a, b, rhs_lanes=False):
    dims = (((1,), (1 if rhs_lanes else 0,)), ((), ()))
    return lax.dot_general(a, b, dims, preferred_element_type=jnp.float32)


def mm(a, b, rhs_lanes=False):
    return dot(a[0], b[0], rhs_lanes) + (dot(a[0], b[1], rhs_lanes) + dot(a[1], b[0], rhs_lanes))


def summary_lines():
    shape = (24, N)
    row = lax.broadcasted_iota(jnp.int32, shape, 0)
    n = lax.broadcasted_iota(jnp.int32, shape, 1)
    part = lax.rem(row, 8)
    pairs = [(d / s, f / s) for s in SCALES for _, _, d, f in DERICHE_POLES]
    rate, freq = (
        jnp.where(
            part < 4,
            jnp.where(part < 2, pairs[0][i], pairs[1][i]),
            jnp.where(part < 6, pairs[2][i], pairs[3][i]),
        )
        for i in range(2)
    )
    steps = jnp.where(row < 8, N - 1 - n, n).astype(jnp.float32)
    angle = freq * steps - jnp.where(lax.rem(row, 2) == 1, math.pi / 2, 0.0)
    square = angle * angle
    cosine = jnp.full(shape, 1.0 / math.factorial(18), jnp.float32)
    for k in range(8, -1, -1):
        cosine = 1.0 / math.factorial(2 * k) - cosine * square
    wave = jnp.exp(-rate * steps) * cosine
    cell = jnp.where(row < 12, row - 8, row + N - 16)
    pick = jnp.where(n == cell, 1.0, 0.0)
    return jnp.where((row >= 8) & (row < 16), pick, wave)


def kernel(
    count,
    x_hbm,
    tab_hbm,
    o_ref,
    x_ref,
    loc_ref,
    ext_ref,
    cv_ref,
    ch_ref,
    pv_ref,
    ph_ref,
    pb_ref,
    gv_ref,
    gh_ref,
    gb_ref,
    acc_ref,
    in_sems,
    send_sems,
    recv_sems,
    late_sem,
    mirror_sem,
    near_sem,
    row_sem,
    ok_sem,
):
    me_r, me_c = lax.axis_index("row"), lax.axis_index("col")
    part = count // 2
    half, spot = me_c // part, lax.rem(me_c, part)
    span = count * 16

    def load(k, src, dst):
        return pltpu.make_async_copy(src, dst, in_sems.at[k])

    def comb_at(pos):
        return tab_hbm.at[pl.ds(pl.multiple_of(COMB_AT + pos * 2 * EXT, 16), 2 * EXT)]

    image, *loads = [
        load(4, x_hbm, x_ref),
        load(0, comb_at(me_c), ch_ref),
        load(1, comb_at(me_r), cv_ref),
        load(2, tab_hbm.at[pl.ds(LOC_AT, 6 * N)], loc_ref),
        load(3, tab_hbm.at[pl.ds(EXT_AT, 6 * N)], ext_ref),
    ]
    image.start()

    early = (0, 1, 2, 3, 4, 5, 6, 7)
    late = (0, 4, 3, 5, 2, 6, 1, 7)

    def near(d):
        return half * part + lax.rem(spot + d, part)

    def far(d):
        return (1 - half) * part + lax.rem(spot + d, part)

    barrier = pltpu.get_barrier_semaphore()

    def greet(sem, row, col):
        pl.semaphore_signal(sem, inc=1, device_id=(row, col), device_id_type=MESH)

    @pl.when(half == 0)
    def _():
        for d in range(part):
            greet(barrier, me_r, far(d))
        for d in range(1, part):
            greet(barrier, me_r, near(d))
        for d in range(1, count):
            greet(barrier, lax.rem(me_r + d, count), me_c)

    mirror = count - 2 - me_c // 2 * 2 + lax.rem(me_c, 2)

    @pl.when(half == 1)
    def _():
        pl.semaphore_wait(barrier, part)
        for d in late:
            greet(late_sem, me_r, far(d))
        greet(mirror_sem, me_r, mirror)

    for copy in loads:
        copy.start()

    def message(kind, k, to, src, dst):
        me = me_c if kind == 0 else me_r
        off = pl.multiple_of(((me - to + count - 1) // count) * 8, 8)
        return pltpu.make_async_remote_copy(
            src_ref=src.at[pl.ds(off, 16)],
            dst_ref=dst.at[pl.ds(pl.multiple_of(me * 16, 16), 16)],
            send_sem=send_sems.at[kind, k],
            recv_sem=recv_sems.at[kind, k],
            device_id=(me_r, to) if kind == 0 else (to, me_c),
            device_id_type=MESH,
        )

    order = sorted(range(1, count), key=lambda d: -min(d, count - d))

    def send_near(ways):
        for d in ways[1:]:
            message(0, d, near(d), ph_ref, gh_ref).start()

    def send_far(ways):
        for d in ways:
            message(0, part + d, far(d), ph_ref, gh_ref).start()

    def send_rows(kind, src, dst):
        for d in order:
            message(kind, d, lax.rem(me_r + d, count), src, dst).start()

    def received(kind, dst):
        for d in range(1, count):
            pltpu.make_async_copy(dst.at[:16], dst.at[:16], recv_sems.at[kind, d]).wait()

    image.wait()
    x = split(x_ref[...])
    m = split(summary_lines())
    ph = mm(m, x, True)
    ph_ref[...] = ph
    gh_ref[pl.ds(pl.multiple_of(me_c * 16, 16), 16), :] = ph[:16]
    pv = mm(m, x)
    pv_ref[...] = pv
    gv_ref[pl.ds(pl.multiple_of(me_r * 16, 16), 16), :] = pv[:16]

    @pl.when(half == 0)
    def _():
        pl.semaphore_wait(barrier, count - 1 + part - 1)
        send_near(early)
        send_rows(1, pv_ref, gv_ref)
        pl.semaphore_wait(mirror_sem, 1)
        for d in range(1, count):
            greet(row_sem, lax.rem(me_r + d, count), me_c)
        pl.semaphore_wait(late_sem, part)

        @pl.when(me_c // 2 == 0)
        def _():
            greet(near_sem, me_r, me_c + count - 4)
            greet(near_sem, me_r, me_c + count - 2)

        @pl.when(me_c // 2 == part // 2 - 1)
        def _():
            greet(near_sem, me_r, me_c + 2)
            greet(near_sem, me_r, me_c + 4)

        send_far(late)
        pl.semaphore_wait(row_sem, count - 1)
        greet(ok_sem, me_r, mirror)

    @pl.when(half == 1)
    def _():
        send_far(early)
        pl.semaphore_wait(near_sem, 1)
        send_near(late)
        pl.semaphore_wait(ok_sem, 1)
        send_rows(1, pv_ref, gv_ref)

    def stacked(v):
        return jnp.concatenate([v[0], v[1], v[0], v[1]], axis=0)

    def paired(v):
        high = v.astype(jnp.bfloat16).astype(jnp.float32)
        lane = lax.broadcasted_iota(jnp.int32, v.shape, 1)
        pair = jnp.where(lane < EXT, high, v - high).astype(jnp.bfloat16)
        return jnp.concatenate([pair, pair], axis=1)

    def combine(c_ref, g_ref):
        return mm((c_ref[:EXT], c_ref[EXT:]), split(g_ref[...]))

    loads[0].wait()
    received(0, gh_ref)
    lines = combine(ch_ref, gh_ref)
    lines = split(jnp.concatenate([lines, lines], axis=0))
    pb = mm(m, lines, True)
    pb_ref[...] = pb
    gb_ref[pl.ds(pl.multiple_of(me_r * 16, 16), 16), :] = pb[:16]
    send_rows(2, pb_ref, gb_ref)
    for k in (1, 2, 3):
        loads[k].wait()
    filtered = dot(loc_ref[...], jnp.concatenate([x[0], x[0]], axis=0)) + dot(loc_ref[:, :N], x[1])
    received(1, gv_ref)
    filtered = filtered + dot(ext_ref[...], stacked(split(combine(cv_ref, gv_ref))))
    pair = paired(mm((loc_ref[:, :N], loc_ref[:, N:]), lines, True))
    for level in range(2):
        for a in range(3):
            k = level * 3 + a
            rows = slice(k * N, (k + 1) * N)
            wide = slice(level * 3 * N, (level * 3 + 3 - a) * N)
            t = split(filtered[rows])
            acc_ref[k, :, : (3 - a) * N] = (
                dot(jnp.concatenate([t[0], t[0]], axis=1), loc_ref[wide], True)
                + dot(t[1], loc_ref[wide, :N], True)
                + dot(pair[rows], ext_ref[wide], True)
            )

    received(2, gb_ref)
    corner = stacked(split(dot(paired(combine(cv_ref, gb_ref)), ext_ref[...], True)))
    for level in range(2):
        for b in range(3):
            k = level * 3 + b
            tall = slice(level * 3 * N, (level * 3 + 3 - b) * N)
            added = dot(ext_ref[tall], corner[:, k * N : (k + 1) * N])
            for a in range(3 - b):
                full = acc_ref[level * 3 + a, :, b * N : (b + 1) * N] + added[a * N : (a + 1) * N]
                o_ref[level * 6 + FEATURES.index((a, b))] = full.astype(jnp.bfloat16)
    for kind, src in enumerate((ph_ref, pv_ref, pb_ref)):
        for d in range(1, count):
            pltpu.make_async_copy(src.at[:16], src.at[:16], send_sems.at[kind, d]).wait()


def on_device(count, table, image):
    f32, bf16 = jnp.float32, jnp.bfloat16
    span = count * 16
    return pl.pallas_call(
        functools.partial(kernel, count),
        out_shape=jax.ShapeDtypeStruct((12, N, N), bf16),
        in_specs=[pl.BlockSpec(memory_space=pltpu.HBM), pl.BlockSpec(memory_space=pl.ANY)],
        out_specs=pl.BlockSpec(memory_space=pltpu.VMEM),
        scratch_shapes=[
            pltpu.VMEM((N, N), f32),
            pltpu.VMEM((6 * N, 256), bf16),
            pltpu.VMEM((6 * N, 256), bf16),
            pltpu.VMEM((2 * EXT, span), bf16),
            pltpu.VMEM((2 * EXT, span), bf16),
            pltpu.VMEM((24, N), f32),
            pltpu.VMEM((24, N), f32),
            pltpu.VMEM((24, N), f32),
            pltpu.VMEM((span, N), f32),
            pltpu.VMEM((span, N), f32),
            pltpu.VMEM((span, N), f32),
            pltpu.VMEM((6, N, 3 * N), f32),
            pltpu.SemaphoreType.DMA((5,)),
            pltpu.SemaphoreType.DMA((3, count)),
            pltpu.SemaphoreType.DMA((3, count)),
            pltpu.SemaphoreType.REGULAR,
            pltpu.SemaphoreType.REGULAR,
            pltpu.SemaphoreType.REGULAR,
            pltpu.SemaphoreType.REGULAR,
            pltpu.SemaphoreType.REGULAR,
        ],
        compiler_params=pltpu.CompilerParams(
            collective_id=0, has_side_effects=True, vmem_limit_bytes=VMEM_LIMIT
        ),
    )(pltpu.with_memory_space_constraint(image, pltpu.HBM), jnp.asarray(table))


VMEM_LIMIT = 54000 << 10


def solution(mesh):
    count = mesh.shape["row"]
    return jax.shard_map(
        functools.partial(on_device, count, packed_table(count)),
        mesh=mesh,
        in_specs=(P("row", "col"),),
        out_specs=P(None, "row", "col"),
        check_vma=False,
    )
```

```python
import functools
import math

import jax
import jax.numpy as jnp
import numpy as np
from jax import lax
from jax.experimental import pallas as pl
from jax.experimental.pallas import tpu as pltpu
from jax.sharding import PartitionSpec as P

SCALES = (128, 256)
DER_FIRST = (1.0 / 280, -4.0 / 105, 1.0 / 5, -4.0 / 5, 0.0, 4.0 / 5, -1.0 / 5, 4.0 / 105, -1.0 / 280)
DER_SECOND = (-1.0 / 560, 8.0 / 315, -1.0 / 5, 8.0 / 5, -205.0 / 72, 8.0 / 5, -1.0 / 5, 8.0 / 315, -1.0 / 560)
DER_NONE = (0.0, 0.0, 0.0, 0.0, 1.0, 0.0, 0.0, 0.0, 0.0)
DERS = (DER_NONE, DER_FIRST, DER_SECOND)
DERICHE_POLES = ((1.68, 3.735, 1.783, 0.6318), (-0.6803, -0.2598, 1.723, 1.997))
FEATURES = ((0, 0), (0, 1), (1, 0), (0, 2), (1, 1), (2, 0))
N = 128
EXT = 64
MESH = pl.DeviceIdType.MESH


def poles(deviation):
    total = 0.0
    for cw, sw, decay, freq in DERICHE_POLES:
        z = np.exp(complex(-decay, freq) / deviation)
        q = z / (1.0 - z)
        total += cw + 2.0 * (cw * q.real + sw * q.imag)
    return [
        (complex(cw, -sw) / total, np.exp(complex(-decay, freq) / deviation))
        for cw, sw, decay, freq in DERICHE_POLES
    ]


def kernel_values(deviation, offsets):
    offsets = np.abs(np.asarray(offsets, dtype=np.float64))
    return sum((a * z**offsets).real for a, z in poles(deviation))


def summary_table():
    table = np.zeros((24, N))
    n = np.arange(N)
    row = 0
    for s in SCALES:
        for _, z in poles(s):
            causal, anti = z ** (N - 1 - n), z**n
            table[row], table[row + 1] = causal.real, causal.imag
            table[16 + row], table[17 + row] = anti.real, anti.imag
            row += 2
    for k in range(4):
        table[8 + k, k] = 1.0
        table[12 + k, N - 4 + k] = 1.0
    return table


def combine_table(count):
    table = np.zeros((count, EXT, count * 16))
    for pos in range(count):
        w = table[pos]
        for k in range(4):
            if pos > 0:
                w[k, (pos - 1) * 16 + 8 + 4 + k] = 1.0
            if pos < count - 1:
                w[4 + k, (pos + 1) * 16 + k] = 1.0
        for si, s in enumerate(SCALES):
            for ai, der in enumerate(DERS):
                for pi, (_, z) in enumerate(poles(s)):
                    up = 8 + (si * 3 + ai) * 8 + pi * 2
                    down = up + 4
                    col = si * 4 + pi * 2
                    dz = sum(der[t + 4] * z**t for t in range(-4, 5))
                    dinv = sum(der[t + 4] * z ** (-t) for t in range(-4, 5))
                    for src in range(count):
                        if src < pos:
                            g = dz * z ** (N * (pos - 1 - src))
                            at = src * 16 + col
                            w[up, at], w[up, at + 1] = g.real, -g.imag
                            w[up + 1, at], w[up + 1, at + 1] = g.imag, g.real
                        if src > pos:
                            g = dinv * z ** (N * (src - pos - 1))
                            at = src * 16 + 8 + col
                            w[down, at], w[down, at + 1] = g.real, -g.imag
                            w[down + 1, at], w[down + 1, at + 1] = g.imag, g.real
                    first = 8
                    last = (count - 1) * 16 + (8 + 4 if pos == count - 1 else 4)
                    for n in range(4):
                        g = -sum(
                            der[n - m + 4] * z ** (N * pos - 1 - m)
                            for m in range(-4, 0)
                            if -4 <= n - m <= 4
                        )
                        w[up, first + n] += g.real
                        w[up + 1, first + n] += g.imag
                        g = -sum(
                            der[n - 4 - m + 4] * z ** (N * (count - 1 - pos) + m)
                            for m in range(0, 4)
                            if -4 <= n - 4 - m <= 4
                        )
                        w[down, last + n] += g.real
                        w[down + 1, last + n] += g.imag
    return table


def filter_tables():
    local = np.zeros((6, N, N))
    ext = np.zeros((6, N, EXT))
    c = np.arange(N)
    for si, s in enumerate(SCALES):
        base = 2.0 * math.sqrt(math.pi) * s
        for ai, der in enumerate(DERS):
            k = si * 3 + ai
            factor = math.sqrt(base) * float(s) ** ai

            def kappa(d):
                return sum(der[t + 4] * kernel_values(s, d + t) for t in range(-4, 5))

            local[k] = kappa(c[:, None] - c[None, :])
            for n in range(4):
                up, down = n - 4, N + n
                ext[k, :, n] = kappa(c - up)
                ext[k, :, 4 + n] = kappa(c - down)
                for a, z in poles(s):
                    dz = sum(der[t + 4] * z**t for t in range(-4, 5))
                    dinv = sum(der[t + 4] * z ** (-t) for t in range(-4, 5))
                    ext[k, :, n] -= (a * dz * z ** (c - up + 0.0)).real
                    ext[k, :, 4 + n] -= (a * dinv * z ** (down - c + 0.0)).real
                ext[k, 4:, n] = 0.0
                ext[k, : N - 4, 4 + n] = 0.0
            for pi, (a, z) in enumerate(poles(s)):
                up = 8 + k * 8 + pi * 2
                g = a * z ** (c + 1.0)
                ext[k, :, up], ext[k, :, up + 1] = g.real, -g.imag
                g = a * z ** (N - c + 0.0)
                ext[k, :, up + 4], ext[k, :, up + 5] = g.real, -g.imag
            local[k] *= factor
            ext[k] *= factor
    return local.reshape(6 * N, N), ext.reshape(6 * N, EXT)


def halves(table):
    table = np.asarray(table, dtype=np.float32)
    high = table.astype(jnp.bfloat16)
    low = (table - high.astype(np.float32)).astype(jnp.bfloat16)
    return high, low


def packed_table(count):
    local, ext = (halves(t) for t in filter_tables())
    comb = halves(combine_table(count))
    return np.concatenate(
        [
            np.concatenate(local, axis=1),
            np.concatenate([ext[0], ext[0], ext[1], ext[1]], axis=1),
            np.concatenate(comb, axis=1).reshape(count * 2 * EXT, count * 16),
        ]
    )


LOC_AT, EXT_AT, COMB_AT = 0, 6 * N, 12 * N


def split(x):
    high = x.astype(jnp.bfloat16)
    return high, (x - high.astype(jnp.float32)).astype(jnp.bfloat16)


def dot(a, b, rhs_lanes=False):
    dims = (((1,), (1 if rhs_lanes else 0,)), ((), ()))
    return lax.dot_general(a, b, dims, preferred_element_type=jnp.float32)


def mm(a, b, rhs_lanes=False):
    return dot(a[0], b[0], rhs_lanes) + (dot(a[0], b[1], rhs_lanes) + dot(a[1], b[0], rhs_lanes))


def summary_lines():
    shape = (24, N)
    row = lax.broadcasted_iota(jnp.int32, shape, 0)
    n = lax.broadcasted_iota(jnp.int32, shape, 1)
    part = lax.rem(row, 8)
    pairs = [(d / s, f / s) for s in SCALES for _, _, d, f in DERICHE_POLES]
    rate, freq = (
        jnp.where(
            part < 4,
            jnp.where(part < 2, pairs[0][i], pairs[1][i]),
            jnp.where(part < 6, pairs[2][i], pairs[3][i]),
        )
        for i in range(2)
    )
    steps = jnp.where(row < 8, N - 1 - n, n).astype(jnp.float32)
    angle = freq * steps - jnp.where(lax.rem(row, 2) == 1, math.pi / 2, 0.0)
    square = angle * angle
    cosine = jnp.full(shape, 1.0 / math.factorial(18), jnp.float32)
    for k in range(8, -1, -1):
        cosine = 1.0 / math.factorial(2 * k) - cosine * square
    wave = jnp.exp(-rate * steps) * cosine
    cell = jnp.where(row < 12, row - 8, row + N - 16)
    pick = jnp.where(n == cell, 1.0, 0.0)
    return jnp.where((row >= 8) & (row < 16), pick, wave)


def kernel(
    count,
    x_hbm,
    tab_hbm,
    o_ref,
    x_ref,
    loc_ref,
    ext_ref,
    cv_ref,
    ch_ref,
    pv_ref,
    ph_ref,
    pb_ref,
    gv_ref,
    gh_ref,
    gb_ref,
    acc_ref,
    in_sems,
    send_sems,
    recv_sems,
    late_sem,
    mirror_sem,
    near_sem,
    row_sem,
    ok_sem,
):
    me_r, me_c = lax.axis_index("row"), lax.axis_index("col")
    part = count // 2
    half, spot = me_c // part, lax.rem(me_c, part)
    span = count * 16

    def load(k, src, dst):
        return pltpu.make_async_copy(src, dst, in_sems.at[k])

    def comb_at(pos):
        return tab_hbm.at[pl.ds(pl.multiple_of(COMB_AT + pos * 2 * EXT, 16), 2 * EXT)]

    image, *loads = [
        load(4, x_hbm, x_ref),
        load(0, comb_at(me_c), ch_ref),
        load(1, comb_at(me_r), cv_ref),
        load(2, tab_hbm.at[pl.ds(LOC_AT, 6 * N)], loc_ref),
        load(3, tab_hbm.at[pl.ds(EXT_AT, 6 * N)], ext_ref),
    ]
    image.start()

    early = (0, 1, 2, 3, 4, 5, 6, 7)
    late = (0, 4, 3, 5, 2, 6, 1, 7)

    def near(d):
        return half * part + lax.rem(spot + d, part)

    def far(d):
        return (1 - half) * part + lax.rem(spot + d, part)

    barrier = pltpu.get_barrier_semaphore()

    def greet(sem, row, col):
        pl.semaphore_signal(sem, inc=1, device_id=(row, col), device_id_type=MESH)

    @pl.when(half == 0)
    def _():
        for d in range(part):
            greet(barrier, me_r, far(d))
        for d in range(1, part):
            greet(barrier, me_r, near(d))
        for d in range(1, count):
            greet(barrier, lax.rem(me_r + d, count), me_c)

    mirror = count - 2 - me_c // 2 * 2 + lax.rem(me_c, 2)

    @pl.when(half == 1)
    def _():
        pl.semaphore_wait(barrier, part)
        for d in late:
            greet(late_sem, me_r, far(d))
        greet(mirror_sem, me_r, mirror)

    for copy in loads:
        copy.start()

    def message(kind, k, to, src, dst):
        me = me_c if kind == 0 else me_r
        off = pl.multiple_of(((me - to + count - 1) // count) * 8, 8)
        return pltpu.make_async_remote_copy(
            src_ref=src.at[pl.ds(off, 16)],
            dst_ref=dst.at[pl.ds(pl.multiple_of(me * 16, 16), 16)],
            send_sem=send_sems.at[kind, k],
            recv_sem=recv_sems.at[kind, k],
            device_id=(me_r, to) if kind == 0 else (to, me_c),
            device_id_type=MESH,
        )

    order = sorted(range(1, count), key=lambda d: -min(d, count - d))

    def send_near(ways):
        for d in ways[1:]:
            message(0, d, near(d), ph_ref, gh_ref).start()

    def send_far(ways):
        for d in ways:
            message(0, part + d, far(d), ph_ref, gh_ref).start()

    def send_rows(kind, src, dst):
        for d in order:
            message(kind, d, lax.rem(me_r + d, count), src, dst).start()

    def received(kind, dst):
        for d in range(1, count):
            pltpu.make_async_copy(dst.at[:16], dst.at[:16], recv_sems.at[kind, d]).wait()

    image.wait()
    x = split(x_ref[...])
    m = split(summary_lines())
    ph = mm(m, x, True)
    ph_ref[...] = ph
    gh_ref[pl.ds(pl.multiple_of(me_c * 16, 16), 16), :] = ph[:16]
    pv = mm(m, x)
    pv_ref[...] = pv
    gv_ref[pl.ds(pl.multiple_of(me_r * 16, 16), 16), :] = pv[:16]

    @pl.when(half == 0)
    def _():
        pl.semaphore_wait(barrier, count - 1 + part - 1)
        send_near(early)
        pl.semaphore_wait(mirror_sem, 1)
        for d in range(1, count):
            greet(row_sem, lax.rem(me_r + d, count), me_c)
        pl.semaphore_wait(late_sem, part)

        @pl.when(me_c // 2 == 0)
        def _():
            greet(near_sem, me_r, me_c + count - 4)
            greet(near_sem, me_r, me_c + count - 2)

        @pl.when(me_c // 2 == part // 2 - 1)
        def _():
            greet(near_sem, me_r, me_c + 2)
            greet(near_sem, me_r, me_c + 4)

        send_far(late)
        send_rows(1, pv_ref, gv_ref)
        pl.semaphore_wait(row_sem, count - 1)
        greet(ok_sem, me_r, mirror)

    @pl.when(half == 1)
    def _():
        send_far(early)
        pl.semaphore_wait(near_sem, 1)
        send_near(late)
        pl.semaphore_wait(ok_sem, 1)
        send_rows(1, pv_ref, gv_ref)

    def stacked(v):
        return jnp.concatenate([v[0], v[1], v[0], v[1]], axis=0)

    def paired(v):
        high = v.astype(jnp.bfloat16).astype(jnp.float32)
        lane = lax.broadcasted_iota(jnp.int32, v.shape, 1)
        pair = jnp.where(lane < EXT, high, v - high).astype(jnp.bfloat16)
        return jnp.concatenate([pair, pair], axis=1)

    def combine(c_ref, g_ref):
        return mm((c_ref[:EXT], c_ref[EXT:]), split(g_ref[...]))

    loads[0].wait()
    received(0, gh_ref)
    lines = combine(ch_ref, gh_ref)
    lines = split(jnp.concatenate([lines, lines], axis=0))
    pb = mm(m, lines, True)
    pb_ref[...] = pb
    gb_ref[pl.ds(pl.multiple_of(me_r * 16, 16), 16), :] = pb[:16]
    send_rows(2, pb_ref, gb_ref)
    for k in (1, 2, 3):
        loads[k].wait()
    filtered = dot(loc_ref[...], jnp.concatenate([x[0], x[0]], axis=0)) + dot(loc_ref[:, :N], x[1])
    received(1, gv_ref)
    filtered = filtered + dot(ext_ref[...], stacked(split(combine(cv_ref, gv_ref))))
    pair = paired(mm((loc_ref[:, :N], loc_ref[:, N:]), lines, True))
    for level in range(2):
        for a in range(3):
            k = level * 3 + a
            rows = slice(k * N, (k + 1) * N)
            wide = slice(level * 3 * N, (level * 3 + 3 - a) * N)
            t = split(filtered[rows])
            acc_ref[k, :, : (3 - a) * N] = (
                dot(jnp.concatenate([t[0], t[0]], axis=1), loc_ref[wide], True)
                + dot(t[1], loc_ref[wide, :N], True)
                + dot(pair[rows], ext_ref[wide], True)
            )

    received(2, gb_ref)
    corner = stacked(split(dot(paired(combine(cv_ref, gb_ref)), ext_ref[...], True)))
    for level in range(2):
        for b in range(3):
            k = level * 3 + b
            tall = slice(level * 3 * N, (level * 3 + 3 - b) * N)
            added = dot(ext_ref[tall], corner[:, k * N : (k + 1) * N])
            for a in range(3 - b):
                full = acc_ref[level * 3 + a, :, b * N : (b + 1) * N] + added[a * N : (a + 1) * N]
                o_ref[level * 6 + FEATURES.index((a, b))] = full.astype(jnp.bfloat16)
    for kind, src in enumerate((ph_ref, pv_ref, pb_ref)):
        for d in range(1, count):
            pltpu.make_async_copy(src.at[:16], src.at[:16], send_sems.at[kind, d]).wait()


def on_device(count, table, image):
    f32, bf16 = jnp.float32, jnp.bfloat16
    span = count * 16
    return pl.pallas_call(
        functools.partial(kernel, count),
        out_shape=jax.ShapeDtypeStruct((12, N, N), bf16),
        in_specs=[pl.BlockSpec(memory_space=pltpu.HBM), pl.BlockSpec(memory_space=pl.ANY)],
        out_specs=pl.BlockSpec(memory_space=pltpu.VMEM),
        scratch_shapes=[
            pltpu.VMEM((N, N), f32),
            pltpu.VMEM((6 * N, 256), bf16),
            pltpu.VMEM((6 * N, 256), bf16),
            pltpu.VMEM((2 * EXT, span), bf16),
            pltpu.VMEM((2 * EXT, span), bf16),
            pltpu.VMEM((24, N), f32),
            pltpu.VMEM((24, N), f32),
            pltpu.VMEM((24, N), f32),
            pltpu.VMEM((span, N), f32),
            pltpu.VMEM((span, N), f32),
            pltpu.VMEM((span, N), f32),
            pltpu.VMEM((6, N, 3 * N), f32),
            pltpu.SemaphoreType.DMA((5,)),
            pltpu.SemaphoreType.DMA((3, count)),
            pltpu.SemaphoreType.DMA((3, count)),
            pltpu.SemaphoreType.REGULAR,
            pltpu.SemaphoreType.REGULAR,
            pltpu.SemaphoreType.REGULAR,
            pltpu.SemaphoreType.REGULAR,
            pltpu.SemaphoreType.REGULAR,
        ],
        compiler_params=pltpu.CompilerParams(
            collective_id=0, has_side_effects=True, vmem_limit_bytes=VMEM_LIMIT
        ),
    )(pltpu.with_memory_space_constraint(image, pltpu.HBM), jnp.asarray(table))


VMEM_LIMIT = 54000 << 10


def solution(mesh):
    count = mesh.shape["row"]
    return jax.shard_map(
        functools.partial(on_device, count, packed_table(count)),
        mesh=mesh,
        in_specs=(P("row", "col"),),
        out_specs=P(None, "row", "col"),
        check_vma=False,
    )
```
